512 devices in a mesh: segment: 4 (over x_hi, core), seq: 32 (over x_lo, z), dp: 4 (over y).
Axes of the slice: x: 4 (x_hi: 2, x_lo: 2; x = x_hi * 2 + x_lo), y: 4, z: 16, core: 2. Of those that a mesh axis runs over, the one named last changes fastest.
Arguments:
- q_in: bfloat16 [4, 4096, 1536], P('dp', 'seq', 'segment'), may hold values from -128 to 128
- k_in: bfloat16 [4, 4096, 1536], P('dp', 'seq', 'segment'), may hold values from -128 to 128
- v_in: bfloat16 [4, 4096, 1536], P('dp', 'seq', 'segment'), may hold values from -6 to 6
- q_gain: float32 [2, 64], replicated, may hold values from 1.5 to 4
- gate: float32 [768], replicated, may hold values from -6 to 6
- cot: bfloat16 [4, 4096, 768], P('dp', 'seq'), may hold values from -6 to 6
Outputs:
- attn_out: bfloat16 [4, 4096, 1536], P('dp', 'seq', 'segment')
- grad_gate: float32 [768], replicated
The draws below stay inside these ranges and needn't reach their ends.
All inputs are finite; a program needn't handle non-finite values.
Results may differ from the reference program's by a relative error of at most 0.028.
The reference program's roundings to bfloat16 on the way (of `probs`, `residual`, `dscore` and `rgrad`) count: a program that leaves them out, or rounds other values in their place, can miss the bound.
Values may be sent and summed in bfloat16 or wider, within the bound.
A program may use at most 64 MiB of HBM per device.

```python
import math
import jax
import jax.numpy as jnp
from jax import lax

HEADS = 12
HEAD_DIM = 64
WIDTH = 768
SEQLEN = 4096
SAMPLES = 4


def joint_rows(key):
    shape = (SAMPLES, SEQLEN, 2 * HEADS * HEAD_DIM)
    key_keys = jax.random.fold_in(key, 101)
    key_queries = jax.random.fold_in(key, 102)
    keys_rows = jax.random.normal(key_keys, shape, jnp.float32)
    query_rows = jax.random.normal(key_queries, shape, jnp.float32)
    return (jnp.clip(query_rows, -120.0, 120.0), jnp.clip(keys_rows, -120.0, 120.0))


def draw_q_in(key, part):
    return joint_rows(key)[0].astype(jnp.bfloat16)


def draw_k_in(key, part):
    return joint_rows(key)[1].astype(jnp.bfloat16)


def level_of(key, extent, cuts, low, high):
    gain, own = 1.0, jax.random.fold_in(key, 6)
    for dim, blocks in cuts:
        steps = jnp.exp(jax.random.uniform(jax.random.fold_in(own, dim), (blocks,), jnp.float32, low / len(cuts), high / len(cuts)))
        gain = gain * jnp.repeat(steps, extent[dim] // blocks).reshape([-1 if axis == dim else 1 for axis in range(len(extent))])
    return gain


def noise(key, extent, scale, reach, shards=(), dtype=jnp.bfloat16):
    factor_of = level_of(key, extent, shards, -0.22, 0.18) if shards else 1.0
    values = jax.random.normal(key, extent, jnp.float32) * scale * factor_of
    return jnp.minimum(jnp.maximum(values, -reach), reach).astype(dtype)


def setup_inputs(seed: int = 0) -> dict:
    key_of = jax.random.split(jax.random.key(seed), 7)
    q_in = draw_q_in(jax.random.fold_in(key_of[6], 71), 0)
    k_in = draw_k_in(jax.random.fold_in(key_of[6], 71), 0)
    v_in = noise(key_of[2], (SAMPLES, SEQLEN, 2 * WIDTH), 1.0, 6.0, ((0, 4), (1, 32), (2, 4)))
    q_gain = jnp.clip(jnp.exp(jax.random.uniform(key_of[3], (2, HEAD_DIM), jnp.float32, math.log(1.5), math.log(4.0))), 1.5, 4.0)
    gate = noise(key_of[4], (WIDTH,), 1.5, 6.0, (), jnp.float32)
    cot = noise(key_of[5], (SAMPLES, SEQLEN, WIDTH), 1.0, 6.0, ((0, 4), (1, 32)))
    return {"q_in": q_in, "k_in": k_in, "v_in": v_in, "q_gain": q_gain, "gate": gate, "cot": cot}


def split_heads(rows):
    return rows.reshape(rows.shape[0], HEADS, HEAD_DIM).transpose(1, 0, 2)

def merge_heads(stacked):
    return stacked.transpose(1, 0, 2).reshape(stacked.shape[1], HEADS * HEAD_DIM)

def unit_rows(rows):
    values = rows.astype(jnp.float32).reshape(rows.shape[0], HEADS, HEAD_DIM)
    return values * lax.rsqrt(lax.optimization_barrier(jnp.mean(values * values, axis=-1, keepdims=True)) + 1e-06)

def head_forward(query_head, keys_head, values_head):
    scores = jnp.dot(query_head.astype(jnp.float32), keys_head.astype(jnp.float32).T) * HEAD_DIM ** (-0.5)
    peak = lax.optimization_barrier(jnp.max(scores, axis=-1, keepdims=True))
    expd = jnp.exp(scores - peak)
    total = lax.optimization_barrier(jnp.sum(expd, axis=-1, keepdims=True))
    probs = expd.astype(jnp.bfloat16)
    normed = jnp.dot(probs.astype(jnp.float32), values_head.astype(jnp.float32)) / total
    return (normed, probs, total)

def control_forward(query, keys, values):

    def single(pieces):
        return head_forward(pieces[0], pieces[1], pieces[2])[0]
    stacked = lax.map(single, (split_heads(query), split_heads(keys), split_heads(values)))
    return merge_heads(stacked)

def main_pass(query, keys, values, upstream):

    def single(pieces):
        query_head, keys_head, values_head, upstream_head = pieces
        normed, probs, total = head_forward(query_head, keys_head, values_head)
        upstream_wide = upstream_head.astype(jnp.float32)
        dprob = jnp.dot(upstream_wide, values_head.astype(jnp.float32).T)
        delta = lax.optimization_barrier(jnp.sum(upstream_wide * normed, axis=-1, keepdims=True))
        dscore = (probs.astype(jnp.float32) / total * (dprob - delta)).astype(jnp.bfloat16)
        dquery = jnp.dot(dscore.astype(jnp.float32), keys_head.astype(jnp.float32)) * HEAD_DIM ** (-0.5)
        return (normed, dquery)
    normed, dquery = lax.map(single, (split_heads(query), split_heads(keys), split_heads(values), split_heads(upstream)))
    return (merge_heads(normed), merge_heads(dquery))

def reference(q_in, k_in, v_in, q_gain, gate, cot):
    width = HEADS * HEAD_DIM
    gate_grad = jnp.zeros((width,), jnp.float32)
    outputs = []
    for sample in range(SAMPLES):
        unit_c = unit_rows(q_in[sample, :, :width])
        base_c = (unit_c * q_gain[0]).reshape(SEQLEN, width)
        query_c = base_c.astype(jnp.bfloat16)
        normed_c = control_forward(query_c, k_in[sample, :, :width], v_in[sample, :, :width])
        out_c = normed_c.astype(jnp.bfloat16)
        out_c_wide = lax.optimization_barrier(out_c).astype(jnp.float32)
        residual = (gate * out_c_wide).astype(jnp.bfloat16)
        unit_m = unit_rows(q_in[sample, :, width:])
        base_m = (unit_m * q_gain[1]).reshape(SEQLEN, width)
        query_m = (base_m + residual.astype(jnp.float32)).astype(jnp.bfloat16)
        normed_m, dquery_m = main_pass(query_m, k_in[sample, :, width:], v_in[sample, :, width:], cot[sample])
        out_m = normed_m.astype(jnp.bfloat16)
        rgrad = lax.optimization_barrier(dquery_m.astype(jnp.bfloat16)).astype(jnp.float32)
        gate_grad = gate_grad + lax.optimization_barrier(jnp.sum(out_c_wide * rgrad, axis=0))
        outputs.append(jnp.concatenate([out_c, out_m], axis=1))
    return (jnp.stack(outputs), gate_grad)
```

```python
import functools

import jax
import jax.numpy as jnp
from jax import lax
from jax.experimental import pallas as pl
from jax.experimental.pallas import tpu as pltpu
from jax.sharding import PartitionSpec as P

MESH = pl.DeviceIdType.MESH
HD = 64
NH = 3
TOK = 128
NZ = 16
KEYS = 4096
ROWS = 2 * TOK
CHUNK = 512
SCALE = HD ** (-0.5)
f32 = jnp.float32
bf16 = jnp.bfloat16


def kernel(
    q_ref, k_ref, v_ref, gain_ref, gate_ref, cot_ref,
    out_ref, gg_ref,
    pack_kv, pack_q, kv, qc, ac, fo, fp, scores, probs, ar1, ar2, ar3,
    ring_s, ring_r, xkv_s, xkv_r, xq_s, xq_r, ac_s, ac_r, fo_s, fo_r,
    ar1_s, ar1_r, ar2_s, ar2_r, ar3_s, ar3_r,
):
    seg = lax.axis_index("segment")
    seq = lax.axis_index("seq")
    dp = lax.axis_index("dp")
    xl = seq // NZ
    z = seq % NZ
    slot = seg % 2
    is_main = seg >= 2
    right = xl * NZ + (z + 1) % NZ
    left = xl * NZ + (z + NZ - 1) % NZ
    xpart = (1 - xl) * NZ + z
    across = (seg + 2) % 4

    barrier = pltpu.get_barrier_semaphore()
    for n in range(1, NZ):
        pl.semaphore_signal(
            barrier, inc=1, device_id={"seq": xl * NZ + (z + n) % NZ}, device_id_type=MESH
        )
    for n in range(1, 4):
        pl.semaphore_signal(barrier, inc=1, device_id={"dp": (dp + n) % 4}, device_id_type=MESH)
    for n in range(1, 8):
        pl.semaphore_signal(
            barrier,
            inc=1,
            device_id={"segment": (seg + n) % 4, "seq": ((xl + n // 4) % 2) * NZ + z},
            device_id_type=MESH,
        )

    for pair in range(3):
        cols = slice(pair * 128, pair * 128 + 128)
        kt, vt, qt = k_ref[0, :, cols], v_ref[0, :, cols], q_ref[0, :, cols]
        ct = cot_ref[0, :, pl.ds(pl.multiple_of(slot * 384 + pair * 128, 128), 128)]
        pack_kv[2 * pair] = jnp.concatenate([kt[:, :HD], vt[:, :HD]], axis=1)
        pack_kv[2 * pair + 1] = jnp.concatenate([kt[:, HD:], vt[:, HD:]], axis=1)
        pack_q[2 * pair] = jnp.concatenate([qt[:, :HD], ct[:, :HD]], axis=1)
        pack_q[2 * pair + 1] = jnp.concatenate([qt[:, HD:], ct[:, HD:]], axis=1)

    def place(zz, half):
        return pl.ds(pl.multiple_of((zz * 2 + half) * TOK, TOK), TOK)

    ar1[z] = jnp.zeros((8, 128), f32)
    for h in range(NH):
        kv[h, place(z, xl)] = pack_kv[xl * NH + h]
        qc[h, pl.ds(pl.multiple_of(xl * TOK, TOK), TOK)] = pack_q[xl * NH + h]

    pl.semaphore_wait(barrier, 25)

    def xkv_copy(h):
        return pltpu.make_async_remote_copy(
            src_ref=pack_kv.at[(1 - xl) * NH + h], dst_ref=kv.at[h, place(z, xl)],
            send_sem=xkv_s.at[h], recv_sem=xkv_r.at[h],
            device_id={"seq": xpart}, device_id_type=MESH,
        )

    def xq_copy(h):
        return pltpu.make_async_remote_copy(
            src_ref=pack_q.at[(1 - xl) * NH + h],
            dst_ref=qc.at[h, pl.ds(pl.multiple_of(xl * TOK, TOK), TOK)],
            send_sem=xq_s.at[h], recv_sem=xq_r.at[h],
            device_id={"seq": xpart}, device_id_type=MESH,
        )

    def ring_copy(h, zz, o, way):
        where = place(zz, (xl + o) % 2)
        return pltpu.make_async_remote_copy(
            src_ref=kv.at[h, where], dst_ref=kv.at[h, where],
            send_sem=ring_s.at[way, h, zz * 2 + o], recv_sem=ring_r.at[way, h, zz * 2 + o],
            device_id={"seq": right if way == 0 else left}, device_id_type=MESH,
        )

    for h in range(NH):
        xkv_copy(h).start()
    for h in range(NH):
        xq_copy(h).start()

    def at(j, way):
        return (z - j + NZ) % NZ if way == 0 else (z + j) % NZ

    for o in range(2):
        for h in range(NH):
            if o == 1:
                xkv_copy(h).wait_recv()
            for way in range(2):
                ring_copy(h, z, o, way).start()

    def ring_step(j, carry):
        for o in range(2):
            for h in range(NH):
                for way in range(2):
                    ring_copy(h, at(j, way), o, way).wait_recv()

                    @pl.when((j < NZ // 2 - 1) | (way == o))
                    def _():
                        ring_copy(h, at(j, way), o, way).start()
        return carry

    lax.fori_loop(1, NZ // 2, ring_step, 0)
    for h in range(NH):
        for o in range(2):
            ring_copy(h, at(NZ // 2, o), o, o).wait_recv()
    for h in range(NH):
        xq_copy(h).wait_recv()

    zero_half = jnp.zeros((ROWS, HD), bf16)

    def base_of(h, row):
        raw = qc[h][:, :HD].astype(f32)
        unit = raw * lax.rsqrt(jnp.mean(raw * raw, axis=-1, keepdims=True) + 1e-06)
        return unit * gain_ref[row:row + 1, :]

    def forward(h, query, keep):
        wide = jnp.concatenate([query * jnp.asarray(SCALE, bf16), zero_half], axis=1)

        def score_step(c, top):
            cols = pl.ds(pl.multiple_of(c * CHUNK, CHUNK), CHUNK)
            s = lax.dot_general(
                wide, kv[h, cols], (((1,), (1,)), ((), ())), preferred_element_type=f32
            )
            scores[:, cols] = s
            for i in range(CHUNK // 128):
                top = jnp.maximum(top, s[:, i * 128:(i + 1) * 128])
            return top

        top = lax.fori_loop(
            0, KEYS // CHUNK, score_step, jnp.full((ROWS, 128), -jnp.inf, f32)
        )
        peak = jnp.max(top, axis=-1, keepdims=True)

        def value_step(c, carry):
            total, acc = carry
            cols = pl.ds(pl.multiple_of(c * CHUNK, CHUNK), CHUNK)
            e = jnp.exp(scores[:, cols] - peak)
            for i in range(CHUNK // 128):
                total = total + e[:, i * 128:(i + 1) * 128]
            p = e.astype(bf16)
            if keep:
                probs[:, cols] = p
            acc = acc + jnp.dot(p, kv[h, cols], preferred_element_type=f32)
            return total, acc

        total, acc = lax.fori_loop(
            0, KEYS // CHUNK, value_step,
            (jnp.zeros((ROWS, 128), f32), jnp.zeros((ROWS, 128), f32)),
        )
        total = jnp.sum(total, axis=-1, keepdims=True)
        return acc[:, HD:] / total, total

    def ac_copy(h):
        return pltpu.make_async_remote_copy(
            src_ref=fo.at[h], dst_ref=ac.at[h], send_sem=ac_s.at[h], recv_sem=ac_r.at[h],
            device_id={"segment": across}, device_id_type=MESH,
        )

    def fo_copy(h):
        return pltpu.make_async_remote_copy(
            src_ref=fo.at[h], dst_ref=fp.at[h], send_sem=fo_s.at[h], recv_sem=fo_r.at[h],
            device_id={"seq": xpart}, device_id_type=MESH,
        )

    def folded(x):
        return jnp.concatenate([x[:TOK], x[TOK:]], axis=1)

    @pl.when(jnp.logical_not(is_main))
    def _():
        for h in range(NH):
            normed, _ = forward(h, base_of(h, 0).astype(bf16), False)
            fo[h] = folded(normed.astype(bf16))
            ac_copy(h).start()
            fo_copy(h).start()
        for h in range(NH):
            ac_copy(h).wait_send()

    def ar1_copy(n, src):
        return pltpu.make_async_remote_copy(
            src_ref=ar1.at[src], dst_ref=ar1.at[src],
            send_sem=ar1_s.at[n], recv_sem=ar1_r.at[src],
            device_id={"seq": xl * NZ + (z + n) % NZ}, device_id_type=MESH,
        )

    def ar2_copy(n, src):
        return pltpu.make_async_remote_copy(
            src_ref=ar2.at[src], dst_ref=ar2.at[src],
            send_sem=ar2_s.at[n], recv_sem=ar2_r.at[src],
            device_id={"dp": (dp + n) % 4}, device_id_type=MESH,
        )

    def ar3_copy(n, src):
        return pltpu.make_async_remote_copy(
            src_ref=ar3.at[src], dst_ref=ar3.at[src],
            send_sem=ar3_s.at[n], recv_sem=ar3_r.at[src],
            device_id={"segment": (seg + n) % 4, "seq": ((xl + n // 4) % 2) * NZ + z},
            device_id_type=MESH,
        )

    @pl.when(is_main)
    def _():
        for h in range(NH):
            base = base_of(h, 1)
            first = slot * 384 + xl * (NH * HD) + h * HD
            tile = gate_ref[:, pl.ds(pl.multiple_of((first // 128) * 128, 128), 128)]
            gate = jnp.where((xl + h) % 2 == 1, tile[:, HD:], tile[:, :HD])
            ac_copy(h).wait_recv()
            pair = ac[h]
            first_wide = jnp.concatenate([pair[:, :HD], pair[:, HD:]], axis=0).astype(f32)
            residual = (gate * first_wide).astype(bf16)
            query = (base + residual.astype(f32)).astype(bf16)
            normed, total = forward(h, query, True)
            fo[h] = folded(normed.astype(bf16))
            fo_copy(h).start()
            upstream = qc[h][:, HD:]
            wide = jnp.concatenate([zero_half, upstream], axis=1)
            delta = jnp.sum(upstream.astype(f32) * normed, axis=-1, keepdims=True)
            inverse = 1.0 / total

            def back_step(c, acc):
                cols = pl.ds(pl.multiple_of(c * CHUNK, CHUNK), CHUNK)
                block = kv[h, cols]
                dprob = lax.dot_general(
                    wide, block, (((1,), (1,)), ((), ())), preferred_element_type=f32
                )
                ds = (probs[:, cols].astype(f32) * inverse * (dprob - delta)).astype(bf16)
                return acc + jnp.dot(ds, block, preferred_element_type=f32)

            acc = lax.fori_loop(0, KEYS // CHUNK, back_step, jnp.zeros((ROWS, 128), f32))
            rgrad = (acc[:, :HD] * SCALE).astype(bf16).astype(f32)
            part = jnp.sum(first_wide * rgrad, axis=0, keepdims=True)
            ar1[z, h:h + 1, :] = jnp.concatenate([part, part], axis=1)

        for n in range(1, NZ):
            ar1_copy(n, z).start()
        for n in range(1, NZ):
            ar1_copy(n, (z + n) % NZ).wait_recv()
        part = ar1[0]
        for n in range(1, NZ):
            part = part + ar1[n]
        ar2[dp] = part
        for n in range(1, 4):
            ar2_copy(n, dp).start()
        for n in range(1, 4):
            ar2_copy(n, (dp + n) % 4).wait_recv()
        ar3[slot * 2 + xl] = (ar2[0] + ar2[1]) + (ar2[2] + ar2[3])
        for n in range(1, 8):
            ar3_copy(n, slot * 2 + xl).start()
        for n in range(1, 4):
            ar3_copy(n, (slot * 2 + xl + n) % 4).wait_recv()
        for n in range(1, NZ):
            ar1_copy(n, z).wait_send()
        for n in range(1, 4):
            ar2_copy(n, dp).wait_send()
        for n in range(1, 8):
            ar3_copy(n, slot * 2 + xl).wait_send()

    @pl.when(jnp.logical_not(is_main))
    def _():
        for n in range(4):
            ar3_copy(1, n).wait_recv()

    for group in range(4):
        for h in range(NH):
            first = group * NH * HD + h * HD
            low = (first % 128) // HD
            gg_ref[:, first:first + HD] = ar3[group, h:h + 1, low * HD:low * HD + HD]

    for h in range(NH):
        fo_copy(h).wait_recv()

    def assemble(lower, upper, half):
        cut = slice(half * HD, half * HD + HD)
        heads = [lower[h][:, cut] for h in range(NH)] + [upper[h][:, cut] for h in range(NH)]
        for pair in range(3):
            out_ref[0, :, pair * 128:pair * 128 + 128] = jnp.concatenate(
                [heads[2 * pair], heads[2 * pair + 1]], axis=1
            )

    @pl.when(xl == 0)
    def _():
        assemble(fo, fp, 0)

    @pl.when(xl == 1)
    def _():
        assemble(fp, fo, 1)

    for h in range(NH):
        fo_copy(h).wait_send()
        xkv_copy(h).wait_send()
        xq_copy(h).wait_send()

    def drain(j, carry):
        for h in range(NH):
            for o in range(2):
                for way in range(2):
                    @pl.when((j < NZ // 2 - 1) | (way == o))
                    def _():
                        ring_copy(h, at(j, way), o, way).wait_send()
        return carry

    lax.fori_loop(0, NZ // 2, drain, 0)


def local(q_in, k_in, v_in, q_gain, gate, cot):
    vmem = pl.BlockSpec(memory_space=pltpu.VMEM)
    dma = pltpu.SemaphoreType.DMA
    out, gg = pl.pallas_call(
        kernel,
        out_shape=(
            jax.ShapeDtypeStruct(q_in.shape, bf16),
            jax.ShapeDtypeStruct((1, gate.shape[0]), f32),
        ),
        in_specs=[vmem] * 6,
        out_specs=(vmem, vmem),
        scratch_shapes=[
            pltpu.VMEM((2 * NH, TOK, 128), bf16),
            pltpu.VMEM((2 * NH, TOK, 128), bf16),
            pltpu.VMEM((NH, KEYS, 128), bf16),
            pltpu.VMEM((NH, ROWS, 128), bf16),
            pltpu.VMEM((NH, TOK, 128), bf16),
            pltpu.VMEM((NH, TOK, 128), bf16),
            pltpu.VMEM((NH, TOK, 128), bf16),
            pltpu.VMEM((ROWS, KEYS), f32),
            pltpu.VMEM((ROWS, KEYS), bf16),
            pltpu.VMEM((NZ, 8, 128), f32),
            pltpu.VMEM((4, 8, 128), f32),
            pltpu.VMEM((4, 8, 128), f32),
            dma((2, NH, 2 * NZ)), dma((2, NH, 2 * NZ)),
            dma((NH,)), dma((NH,)), dma((NH,)), dma((NH,)),
            dma((NH,)), dma((NH,)), dma((NH,)), dma((NH,)),
            dma((NZ,)), dma((NZ,)), dma((4,)), dma((4,)), dma((8,)), dma((4,)),
        ],
        compiler_params=pltpu.CompilerParams(
            collective_id=0, has_side_effects=True, vmem_limit_bytes=48 * 2**20
        ),
    )(q_in, k_in, v_in, q_gain, gate.reshape(1, -1), cot)
    return out, gg.reshape(-1)


def solution(mesh):
    in_specs = (
        P("dp", "seq", "segment"),
        P("dp", "seq", "segment"),
        P("dp", "seq", "segment"),
        P(),
        P(),
        P("dp", "seq", None),
    )
    out_specs = (P("dp", "seq", "segment"), P())
    return jax.shard_map(local, mesh=mesh, in_specs=in_specs, out_specs=out_specs, check_vma=False)
```

```python
import functools

import jax
import jax.numpy as jnp
from jax import lax
from jax.experimental import pallas as pl
from jax.experimental.pallas import tpu as pltpu
from jax.sharding import PartitionSpec as P

MESH = pl.DeviceIdType.MESH
HD = 64
NH = 3
TOK = 128
NZ = 16
KEYS = 4096
ROWS = 2 * TOK
CHUNK = 4096
SCALE = HD ** (-0.5)
f32 = jnp.float32
bf16 = jnp.bfloat16


def kernel(
    q_hbm, k_hbm, v_hbm, gain_ref, gate_ref, cot_hbm,
    out_ref, gg_ref,
    q_ref, k_ref, v_ref, cot_ref, load_s,
    pack_kv, pack_q, kv, qc, ac, fo, fp, scores, probs, ar1, ar2, ar3,
    ring_s, ring_r, xkv_s, xkv_r, xq_s, xq_r, ac_s, ac_r, fo_s, fo_r,
    ar1_s, ar1_r, ar2_s, ar2_r, ar3_s, ar3_r,
):
    seg = lax.axis_index("segment")
    seq = lax.axis_index("seq")
    dp = lax.axis_index("dp")
    xl = seq // NZ
    z = seq % NZ
    slot = seg % 2
    is_main = seg >= 2
    right = xl * NZ + (z + 1) % NZ
    left = xl * NZ + (z + NZ - 1) % NZ
    xpart = (1 - xl) * NZ + z
    across = (seg + 2) % 4

    loads = [
        pltpu.make_async_copy(src, dst, load_s.at[n])
        for n, (src, dst) in enumerate(
            ((k_hbm, k_ref), (v_hbm, v_ref), (q_hbm, q_ref), (cot_hbm, cot_ref))
        )
    ]
    for load in loads:
        load.start()

    barrier = pltpu.get_barrier_semaphore()
    for n in range(1, NZ):
        pl.semaphore_signal(
            barrier, inc=1, device_id={"seq": xl * NZ + (z + n) % NZ}, device_id_type=MESH
        )
    for n in range(1, 4):
        pl.semaphore_signal(barrier, inc=1, device_id={"dp": (dp + n) % 4}, device_id_type=MESH)
    for n in range(1, 8):
        pl.semaphore_signal(
            barrier,
            inc=1,
            device_id={"segment": (seg + n) % 4, "seq": ((xl + n // 4) % 2) * NZ + z},
            device_id_type=MESH,
        )

    for load in loads:
        load.wait()
    for pair in range(3):
        cols = slice(pair * 128, pair * 128 + 128)
        kt, vt, qt = k_ref[0, :, cols], v_ref[0, :, cols], q_ref[0, :, cols]
        ct = cot_ref[0, :, pl.ds(pl.multiple_of(slot * 384 + pair * 128, 128), 128)]
        pack_kv[2 * pair] = jnp.concatenate([kt[:, :HD], vt[:, :HD]], axis=1)
        pack_kv[2 * pair + 1] = jnp.concatenate([kt[:, HD:], vt[:, HD:]], axis=1)
        pack_q[2 * pair] = jnp.concatenate([qt[:, :HD], ct[:, :HD]], axis=1)
        pack_q[2 * pair + 1] = jnp.concatenate([qt[:, HD:], ct[:, HD:]], axis=1)

    def place(zz, half):
        return pl.ds(pl.multiple_of((zz * 2 + half) * TOK, TOK), TOK)

    ar1[z] = jnp.zeros((8, 128), f32)
    for h in range(NH):
        kv[h, place(z, xl)] = pack_kv[xl * NH + h]
        qc[h, pl.ds(pl.multiple_of(xl * TOK, TOK), TOK)] = pack_q[xl * NH + h]

    pl.semaphore_wait(barrier, 25)

    def xkv_copy(h):
        return pltpu.make_async_remote_copy(
            src_ref=pack_kv.at[(1 - xl) * NH + h], dst_ref=kv.at[h, place(z, xl)],
            send_sem=xkv_s.at[h], recv_sem=xkv_r.at[h],
            device_id={"seq": xpart}, device_id_type=MESH,
        )

    def xq_copy(h):
        return pltpu.make_async_remote_copy(
            src_ref=pack_q.at[(1 - xl) * NH + h],
            dst_ref=qc.at[h, pl.ds(pl.multiple_of(xl * TOK, TOK), TOK)],
            send_sem=xq_s.at[h], recv_sem=xq_r.at[h],
            device_id={"seq": xpart}, device_id_type=MESH,
        )

    def ring_copy(h, zz, o, way):
        where = place(zz, (xl + o) % 2)
        return pltpu.make_async_remote_copy(
            src_ref=kv.at[h, where], dst_ref=kv.at[h, where],
            send_sem=ring_s.at[way, h, zz * 2 + o], recv_sem=ring_r.at[way, h, zz * 2 + o],
            device_id={"seq": right if way == 0 else left}, device_id_type=MESH,
        )

    for h in range(NH):
        xkv_copy(h).start()
    for h in range(NH):
        xq_copy(h).start()

    def at(j, way):
        return (z - j + NZ) % NZ if way == 0 else (z + j) % NZ

    for o in range(2):
        for h in range(NH):
            if o == 1:
                xkv_copy(h).wait_recv()
            for way in range(2):
                ring_copy(h, z, o, way).start()

    def ring_step(j, carry):
        for o in range(2):
            for h in range(NH):
                for way in range(2):
                    ring_copy(h, at(j, way), o, way).wait_recv()

                    @pl.when((j < NZ // 2 - 1) | (way == o))
                    def _():
                        ring_copy(h, at(j, way), o, way).start()
        return carry

    lax.fori_loop(1, NZ // 2, ring_step, 0)
    for h in range(NH):
        for o in range(2):
            ring_copy(h, at(NZ // 2, o), o, o).wait_recv()
    for h in range(NH):
        xq_copy(h).wait_recv()

    zero_half = jnp.zeros((ROWS, HD), bf16)

    def base_of(h, row):
        raw = qc[h][:, :HD].astype(f32)
        unit = raw * lax.rsqrt(jnp.mean(raw * raw, axis=-1, keepdims=True) + 1e-06)
        return unit * gain_ref[row:row + 1, :]

    def forward(h, query, keep):
        wide = jnp.concatenate([query * jnp.asarray(SCALE, bf16), zero_half], axis=1)

        def score_step(c, top):
            cols = pl.ds(pl.multiple_of(c * CHUNK, CHUNK), CHUNK)
            s = lax.dot_general(
                wide, kv[h, cols], (((1,), (1,)), ((), ())), preferred_element_type=f32
            )
            scores[:, cols] = s
            for i in range(CHUNK // 128):
                top = jnp.maximum(top, s[:, i * 128:(i + 1) * 128])
            return top

        top = lax.fori_loop(
            0, KEYS // CHUNK, score_step, jnp.full((ROWS, 128), -jnp.inf, f32)
        )
        peak = jnp.max(top, axis=-1, keepdims=True)

        def value_step(c, carry):
            total, acc = carry
            cols = pl.ds(pl.multiple_of(c * CHUNK, CHUNK), CHUNK)
            e = jnp.exp(scores[:, cols] - peak)
            for i in range(CHUNK // 128):
                total = total + e[:, i * 128:(i + 1) * 128]
            p = e.astype(bf16)
            if keep:
                probs[:, cols] = p
            acc = acc + jnp.dot(p, kv[h, cols], preferred_element_type=f32)
            return total, acc

        total, acc = lax.fori_loop(
            0, KEYS // CHUNK, value_step,
            (jnp.zeros((ROWS, 128), f32), jnp.zeros((ROWS, 128), f32)),
        )
        total = jnp.sum(total, axis=-1, keepdims=True)
        return acc[:, HD:] / total, total

    def ac_copy(h):
        return pltpu.make_async_remote_copy(
            src_ref=fo.at[h], dst_ref=ac.at[h], send_sem=ac_s.at[h], recv_sem=ac_r.at[h],
            device_id={"segment": across}, device_id_type=MESH,
        )

    def fo_copy(h):
        return pltpu.make_async_remote_copy(
            src_ref=fo.at[h], dst_ref=fp.at[h], send_sem=fo_s.at[h], recv_sem=fo_r.at[h],
            device_id={"seq": xpart}, device_id_type=MESH,
        )

    def folded(x):
        return jnp.concatenate([x[:TOK], x[TOK:]], axis=1)

    @pl.when(jnp.logical_not(is_main))
    def _():
        def control_head(h, carry):
            normed, _ = forward(h, base_of(h, 0).astype(bf16), False)
            fo[h] = folded(normed.astype(bf16))
            ac_copy(h).start()
            fo_copy(h).start()
            return carry

        lax.fori_loop(0, NH, control_head, 0)
        for h in range(NH):
            ac_copy(h).wait_send()

    def ar1_copy(n, src):
        return pltpu.make_async_remote_copy(
            src_ref=ar1.at[src], dst_ref=ar1.at[src],
            send_sem=ar1_s.at[n], recv_sem=ar1_r.at[src],
            device_id={"seq": xl * NZ + (z + n) % NZ}, device_id_type=MESH,
        )

    def ar2_copy(n, src):
        return pltpu.make_async_remote_copy(
            src_ref=ar2.at[src], dst_ref=ar2.at[src],
            send_sem=ar2_s.at[n], recv_sem=ar2_r.at[src],
            device_id={"dp": (dp + n) % 4}, device_id_type=MESH,
        )

    def ar3_copy(n, src):
        return pltpu.make_async_remote_copy(
            src_ref=ar3.at[src], dst_ref=ar3.at[src],
            send_sem=ar3_s.at[n], recv_sem=ar3_r.at[src],
            device_id={"segment": (seg + n) % 4, "seq": ((xl + n // 4) % 2) * NZ + z},
            device_id_type=MESH,
        )

    @pl.when(is_main)
    def _():
        def main_head(h, carry):
            base = base_of(h, 1)
            first = slot * 384 + xl * (NH * HD) + h * HD
            tile = gate_ref[:, pl.ds(pl.multiple_of((first // 128) * 128, 128), 128)]
            gate = jnp.where((xl + h) % 2 == 1, tile[:, HD:], tile[:, :HD])
            ac_copy(h).wait_recv()
            pair = ac[h]
            first_wide = jnp.concatenate([pair[:, :HD], pair[:, HD:]], axis=0).astype(f32)
            residual = (gate * first_wide).astype(bf16)
            query = (base + residual.astype(f32)).astype(bf16)
            normed, total = forward(h, query, True)
            fo[h] = folded(normed.astype(bf16))
            fo_copy(h).start()
            upstream = qc[h][:, HD:]
            wide = jnp.concatenate([zero_half, upstream], axis=1)
            delta = jnp.sum(upstream.astype(f32) * normed, axis=-1, keepdims=True)
            inverse = 1.0 / total

            def back_step(c, acc):
                cols = pl.ds(pl.multiple_of(c * CHUNK, CHUNK), CHUNK)
                block = kv[h, cols]
                dprob = lax.dot_general(
                    wide, block, (((1,), (1,)), ((), ())), preferred_element_type=f32
                )
                ds = (probs[:, cols].astype(f32) * inverse * (dprob - delta)).astype(bf16)
                return acc + jnp.dot(ds, block, preferred_element_type=f32)

            acc = lax.fori_loop(0, KEYS // CHUNK, back_step, jnp.zeros((ROWS, 128), f32))
            rgrad = (acc[:, :HD] * SCALE).astype(bf16).astype(f32)
            part = jnp.sum(first_wide * rgrad, axis=0, keepdims=True)
            ar1[z, pl.ds(h, 1), :] = jnp.concatenate([part, part], axis=1)
            return carry

        lax.fori_loop(0, NH, main_head, 0)

        for n in range(1, NZ):
            ar1_copy(n, z).start()
        for n in range(1, NZ):
            ar1_copy(n, (z + n) % NZ).wait_recv()
        part = ar1[0]
        for n in range(1, NZ):
            part = part + ar1[n]
        ar2[dp] = part
        for n in range(1, 4):
            ar2_copy(n, dp).start()
        for n in range(1, 4):
            ar2_copy(n, (dp + n) % 4).wait_recv()
        ar3[slot * 2 + xl] = (ar2[0] + ar2[1]) + (ar2[2] + ar2[3])
        for n in range(1, 8):
            ar3_copy(n, slot * 2 + xl).start()
        for n in range(1, 4):
            ar3_copy(n, (slot * 2 + xl + n) % 4).wait_recv()
        for n in range(1, NZ):
            ar1_copy(n, z).wait_send()
        for n in range(1, 4):
            ar2_copy(n, dp).wait_send()
        for n in range(1, 8):
            ar3_copy(n, slot * 2 + xl).wait_send()

    @pl.when(jnp.logical_not(is_main))
    def _():
        for n in range(4):
            ar3_copy(1, n).wait_recv()

    for group in range(4):
        for h in range(NH):
            first = group * NH * HD + h * HD
            low = (first % 128) // HD
            gg_ref[:, first:first + HD] = ar3[group, h:h + 1, low * HD:low * HD + HD]

    for h in range(NH):
        fo_copy(h).wait_recv()

    def assemble(lower, upper, half):
        cut = slice(half * HD, half * HD + HD)
        heads = [lower[h][:, cut] for h in range(NH)] + [upper[h][:, cut] for h in range(NH)]
        for pair in range(3):
            out_ref[0, :, pair * 128:pair * 128 + 128] = jnp.concatenate(
                [heads[2 * pair], heads[2 * pair + 1]], axis=1
            )

    @pl.when(xl == 0)
    def _():
        assemble(fo, fp, 0)

    @pl.when(xl == 1)
    def _():
        assemble(fp, fo, 1)

    for h in range(NH):
        fo_copy(h).wait_send()
        xkv_copy(h).wait_send()
        xq_copy(h).wait_send()

    def drain(j, carry):
        for h in range(NH):
            for o in range(2):
                for way in range(2):
                    @pl.when((j < NZ // 2 - 1) | (way == o))
                    def _():
                        ring_copy(h, at(j, way), o, way).wait_send()
        return carry

    lax.fori_loop(0, NZ // 2, drain, 0)


def local(q_in, k_in, v_in, q_gain, gate, cot):
    hbm = pl.BlockSpec(memory_space=pltpu.HBM)
    vmem = pl.BlockSpec(memory_space=pltpu.VMEM)
    dma = pltpu.SemaphoreType.DMA
    out, gg = pl.pallas_call(
        kernel,
        out_shape=(
            jax.ShapeDtypeStruct(q_in.shape, bf16),
            jax.ShapeDtypeStruct((1, gate.shape[0]), f32),
        ),
        in_specs=[hbm] * 3 + [vmem] * 2 + [hbm],
        out_specs=(vmem, vmem),
        scratch_shapes=[
            pltpu.VMEM(q_in.shape, bf16),
            pltpu.VMEM(k_in.shape, bf16),
            pltpu.VMEM(v_in.shape, bf16),
            pltpu.VMEM(cot.shape, bf16),
            pltpu.SemaphoreType.DMA((4,)),
            pltpu.VMEM((2 * NH, TOK, 128), bf16),
            pltpu.VMEM((2 * NH, TOK, 128), bf16),
            pltpu.VMEM((NH, KEYS, 128), bf16),
            pltpu.VMEM((NH, ROWS, 128), bf16),
            pltpu.VMEM((NH, TOK, 128), bf16),
            pltpu.VMEM((NH, TOK, 128), bf16),
            pltpu.VMEM((NH, TOK, 128), bf16),
            pltpu.VMEM((ROWS, KEYS), f32),
            pltpu.VMEM((ROWS, KEYS), bf16),
            pltpu.VMEM((NZ, 8, 128), f32),
            pltpu.VMEM((4, 8, 128), f32),
            pltpu.VMEM((4, 8, 128), f32),
            dma((2, NH, 2 * NZ)), dma((2, NH, 2 * NZ)),
            dma((NH,)), dma((NH,)), dma((NH,)), dma((NH,)),
            dma((NH,)), dma((NH,)), dma((NH,)), dma((NH,)),
            dma((NZ,)), dma((NZ,)), dma((4,)), dma((4,)), dma((8,)), dma((4,)),
        ],
        compiler_params=pltpu.CompilerParams(
            collective_id=0, has_side_effects=True, vmem_limit_bytes=48 * 2**20
        ),
    )(q_in, k_in, v_in, q_gain, gate.reshape(1, -1), cot)
    return out, gg.reshape(-1)


def solution(mesh):
    in_specs = (
        P("dp", "seq", "segment"),
        P("dp", "seq", "segment"),
        P("dp", "seq", "segment"),
        P(),
        P(),
        P("dp", "seq", None),
    )
    out_specs = (P("dp", "seq", "segment"), P())
    return jax.shard_map(local, mesh=mesh, in_specs=in_specs, out_specs=out_specs, check_vma=False)
```

```python
import functools

import jax
import jax.numpy as jnp
from jax import lax
from jax.experimental import pallas as pl
from jax.experimental.pallas import tpu as pltpu
from jax.sharding import PartitionSpec as P

MESH = pl.DeviceIdType.MESH
HD = 64
NH = 3
TOK = 128
NZ = 16
NQ = 4
NP = 16
KEYS = 4096
ROWS = 2 * TOK
CHUNK = 4096
SCALE = HD ** (-0.5)
f32 = jnp.float32
bf16 = jnp.bfloat16


def kernel(
    q_hbm, k_hbm, v_hbm, gain_ref, gate_ref, cot_hbm,
    out_ref, gg_ref,
    q_ref, k_ref, v_ref, cot_ref,
    pack_kv, pack_q, pack_c, kv, qb, cb, ac, fo, rp, scores, probs, dprob, parts, ar1, ar2,
    load_s, p1_s, p1_r, q_s, q_r, c_s, c_r, ag_s, ag_r, ac_s, ac_r, rp_s, rp_r,
    ar1_s, ar1_r, ar2_s, ar2_r,
):
    seg = lax.axis_index("segment")
    seq = lax.axis_index("seq")
    y = lax.axis_index("dp")
    xh, c = seg // 2, seg % 2
    x, z = seq // NZ, seq % NZ
    is_main = xh == 1
    zq, zs = z // 4, z % 4
    me = (y * 2 + x) * 2 + c
    itself = z == 12 * c + y

    loads = [
        pltpu.make_async_copy(src, dst, load_s.at[n])
        for n, (src, dst) in enumerate(
            ((k_hbm, k_ref), (v_hbm, v_ref), (q_hbm, q_ref), (cot_hbm, cot_ref))
        )
    ]
    for load in loads:
        load.start()

    def target(f):
        return {"segment": xh * 2 + zq % 2, "seq": x * NZ + 4 * (2 * c + f) + y, "dp": zs}

    def source(b):
        return {"segment": xh * 2 + zq // 2, "seq": x * NZ + y + 4 * c + 8 * b, "dp": zs}

    def in_row(p):
        return {"segment": xh * 2 + p % 2, "seq": ((p // 2) % 2) * NZ + z, "dp": p // 4}

    def in_column(n):
        there = (xh * NZ + z + n) % (2 * NZ)
        return {"segment": (there // NZ) * 2 + c, "seq": x * NZ + there % NZ}

    def stays(n):
        return itself & (c == n)

    barrier = pltpu.get_barrier_semaphore()

    def hello(device):
        pl.semaphore_signal(barrier, inc=1, device_id=device, device_id_type=MESH)

    for n in range(2):
        @pl.when(jnp.logical_not(stays(n)))
        def _():
            hello(target(n))
            hello(source(n))
    for n in range(1, NP):
        hello(in_row((me + n) % NP))
    for n in range(1, 2 * NZ):
        hello(in_column(n))

    def fold(a):
        return jnp.concatenate([a[:HD], a[HD:]], axis=1)

    def unfold(a):
        return jnp.concatenate([a[:, :HD], a[:, HD:]], axis=0)

    for load in loads:
        load.wait()
    for pair in range(3):
        cols = slice(pair * 128, pair * 128 + 128)
        kt, vt, qt = k_ref[0, :, cols], v_ref[0, :, cols], q_ref[0, :, cols]
        ct = cot_ref[0, :, pl.ds(pl.multiple_of(c * 384 + pair * 128, 128), 128)]
        for half in range(2):
            f, h = (2 * pair + half) // NH, (2 * pair + half) % NH
            lanes = slice(half * HD, half * HD + HD)
            pack_kv[f, h] = jnp.concatenate([kt[:, lanes], vt[:, lanes]], axis=1)
            pack_q[f, h] = fold(qt[:, lanes])
            pack_c[f, h] = fold(ct[:, lanes])

    def rows(p, b):
        return pl.ds(pl.multiple_of((p * 2 + b) * TOK, TOK), TOK)

    def whole(p):
        return pl.ds(pl.multiple_of(p * ROWS, ROWS), ROWS)

    def remote(src, dst, send, recv, device):
        return pltpu.make_async_remote_copy(
            src_ref=src, dst_ref=dst, send_sem=send, recv_sem=recv,
            device_id=device, device_id_type=MESH,
        )

    there = (zs * 2 + x) * 2 + zq % 2
    block = zq // 2

    def p1_send(h, f):
        return remote(
            pack_kv.at[f, h], kv.at[h, rows(there, block)], p1_s.at[f, h], p1_r.at[block, h],
            target(f),
        )

    def p1_wait(h, b):
        return remote(
            pack_kv.at[0, h], kv.at[h, rows(me, b)], p1_s.at[0, h], p1_r.at[b, h], source(b)
        )

    def q_send(f):
        return remote(pack_q.at[f], qb.at[block], q_s.at[f], q_r.at[block], target(f))

    def q_wait(b):
        return remote(pack_q.at[0], qb.at[b], q_s.at[0], q_r.at[b], source(b))

    def c_send(f):
        return remote(pack_c.at[f], cb.at[block], c_s.at[f], c_r.at[block], target(f))

    def c_wait(b):
        return remote(pack_c.at[0], cb.at[b], c_s.at[0], c_r.at[b], source(b))

    pl.semaphore_wait(barrier, 50 - 2 * itself.astype(jnp.int32))

    for h in range(NH):
        for f in range(2):
            @pl.when(jnp.logical_not(stays(f)))
            def _():
                p1_send(h, f).start()
        if h == NH - 1:
            for f in range(2):
                @pl.when(jnp.logical_not(stays(f)))
                def _():
                    q_send(f).start()
    for f in range(2):
        @pl.when(stays(f))
        def _():
            for h in range(NH):
                kv[h, rows(me, f)] = pack_kv[f, h]
            qb[f] = pack_q[f]
            cb[f] = pack_c[f]

    over_x = {"seq": (1 - x) * NZ + z}
    up, down = {"dp": (y + 1) % 4}, {"dp": (y + 3) % 4}
    sibling = {"segment": xh * 2 + 1 - c}

    def at(dy, dx):
        return (((y + dy) % 4) * 2 + (x + dx) % 2) * 2 + c

    def ag(h, k, p, b, device):
        where = whole(p) if b is None else rows(p, b)
        return remote(
            kv.at[h, where], kv.at[h, where], ag_s.at[h, k], ag_r.at[h, p, b or 0], device
        )

    def arrived(h, p, b=None):
        ag(h, 0, p, b, over_x).wait_recv()

    sends = (
        (0, (0, 0), None, over_x), (0, (0, 0), None, up), (0, (0, 0), None, down),
        (0, (0, 0), None, sibling),
        (1, (0, 1), None, up), (1, (0, 1), None, down), (1, (0, 1), None, sibling),
        (2, (1, 0), 0, down), (2, (1, 0), None, sibling),
        (3, (3, 0), 1, up), (3, (3, 0), None, sibling),
        (4, (1, 1), None, sibling), (5, (3, 1), None, sibling),
        (6, (2, 0), None, over_x), (6, (2, 0), None, sibling),
        (7, (2, 1), None, sibling),
    )

    def stage(h, number):
        if number == 0:
            for b in range(2):
                @pl.when(jnp.logical_not(stays(b)))
                def _():
                    p1_wait(h, b).wait_recv()
        elif number == 6:
            arrived(h, at(2, 0), 0)
            arrived(h, at(2, 0), 1)
        else:
            place = next(s[1] for s in sends if s[0] == number)
            arrived(h, at(*place))
        for k, (n, place, b, device) in enumerate(sends):
            if n == number:
                ag(h, k, at(*place), b, device).start()

    zero_half = jnp.zeros((ROWS, HD), bf16)

    def both(ref, h):
        return jnp.concatenate([unfold(ref[0, h]), unfold(ref[1, h])], axis=0)

    def base_of(h, row):
        raw = both(qb, h).astype(f32)
        unit = raw * lax.rsqrt(jnp.mean(raw * raw, axis=-1, keepdims=True) + 1e-06)
        return unit * gain_ref[row:row + 1, :]

    def forward(h, query, keep):
        wide = jnp.concatenate([query * jnp.asarray(SCALE, bf16), zero_half], axis=1)
        s = lax.dot_general(wide, kv[h], (((1,), (1,)), ((), ())), preferred_element_type=f32)
        scores[...] = s
        top = s[:, :128]
        for i in range(1, KEYS // 128):
            top = jnp.maximum(top, s[:, i * 128:(i + 1) * 128])
        peak = jnp.max(top, axis=-1, keepdims=True)
        e = jnp.exp(scores[...] - peak)
        total = e[:, :128]
        for i in range(1, KEYS // 128):
            total = total + e[:, i * 128:(i + 1) * 128]
        p = e.astype(bf16)
        if keep:
            probs[...] = p
        acc = jnp.dot(p, kv[h], preferred_element_type=f32)
        total = jnp.sum(total, axis=-1, keepdims=True)
        return acc[:, HD:] / total, total

    def ac_copy(h):
        return remote(
            fo.at[h], ac.at[h], ac_s.at[h], ac_r.at[h], {"segment": (1 - xh) * 2 + c}
        )

    def rp_send(h, b):
        return remote(
            fo.at[h, b], rp.at[zq % 2, h], rp_s.at[h, b], rp_r.at[zq % 2, h], source(b)
        )

    def rp_wait(h, f):
        return remote(fo.at[h, 0], rp.at[f, h], rp_s.at[h, 0], rp_r.at[f, h], target(f))

    def give_back(h):
        for b in range(2):
            @pl.when(jnp.logical_not(stays(b)))
            def _():
                rp_send(h, b).start()

            @pl.when(stays(b))
            def _():
                rp[b, h] = fo[h, b]

    def keep_out(h, normed):
        fo[h, 0] = fold(normed[:TOK].astype(bf16))
        fo[h, 1] = fold(normed[TOK:].astype(bf16))

    def control_head(h):
        normed, _ = forward(h, base_of(h, 0).astype(bf16), False)
        keep_out(h, normed)
        ac_copy(h).start()
        give_back(h)

    def dprob_head(h):
        wide = jnp.concatenate([zero_half, both(cb, h)], axis=1)
        dprob[h] = lax.dot_general(
            wide, kv[h], (((1,), (1,)), ((), ())), preferred_element_type=f32
        )

    def main_head(h):
        base = base_of(h, 1)
        first = zq * (NH * HD) + h * HD
        tile = gate_ref[pl.ds(pl.multiple_of((first // 128) * 128, 128), 128)].reshape(1, 128)
        gate = jnp.where((zq + h) % 2 == 1, tile[:, HD:], tile[:, :HD])
        ac_copy(h).wait_recv()
        first_wide = jnp.concatenate([unfold(ac[h, 0]), unfold(ac[h, 1])], axis=0).astype(f32)
        residual = (gate * first_wide).astype(bf16)
        query = (base + residual.astype(f32)).astype(bf16)
        normed, total = forward(h, query, True)
        keep_out(h, normed)
        give_back(h)
        upstream = both(cb, h)
        delta = jnp.sum(upstream.astype(f32) * normed, axis=-1, keepdims=True)
        inverse = 1.0 / total
        ds = (probs[...].astype(f32) * inverse * (dprob[h] - delta)).astype(bf16)
        acc = jnp.dot(ds, kv[h], preferred_element_type=f32)
        rgrad = (acc[:, :HD] * SCALE).astype(bf16).astype(f32)
        part = jnp.sum(first_wide * rgrad, axis=0, keepdims=True)
        parts[pl.ds(h, 1), :] = jnp.concatenate([part, part], axis=1)

    def complete(h):
        for dy in range(4):
            for dx in range(2):
                arrived(h, at(dy, dx) + 1 - 2 * c)

    def stages(h, *numbers):
        for n in numbers:
            stage(h, n)

    stages(0, 0, 1, 2, 3)
    stages(1, 0)
    stages(0, 4, 5, 6)
    stages(1, 1, 2, 3)
    stages(2, 0)
    for f in range(2):
        @pl.when(is_main & jnp.logical_not(stays(f)))
        def _():
            c_send(f).start()
    for b in range(2):
        @pl.when(jnp.logical_not(stays(b)))
        def _():
            q_wait(b).wait_recv()
    stages(1, 4, 5, 6)
    stages(0, 7)
    complete(0)

    @pl.when(is_main)
    def _():
        stages(2, 1, 2, 3)
        stages(1, 7)
        for b in range(2):
            @pl.when(jnp.logical_not(stays(b)))
            def _():
                c_wait(b).wait_recv()
        complete(1)

        def ahead(h, carry):
            dprob_head(h)
            return carry

        lax.fori_loop(0, 2, ahead, 0)

    def heads(h, carry):
        @pl.when(jnp.logical_not(is_main))
        def _():
            @pl.when(h == 1)
            def _():
                stages(2, 1, 2, 3)
                stages(1, 7)
                complete(1)

            @pl.when(h == 2)
            def _():
                stages(2, 4, 5, 6, 7)
                complete(2)

            control_head(h)

        @pl.when(is_main)
        def _():
            @pl.when(h == 1)
            def _():
                stages(2, 4, 5, 6)

            @pl.when(h == 2)
            def _():
                stages(2, 7)
                complete(2)
                dprob_head(2)

            main_head(h)
        return carry

    lax.fori_loop(0, NH, heads, 0)

    def ar1_copy(n, p):
        return remote(
            ar1.at[p], ar1.at[p], ar1_s.at[n], ar1_r.at[p], in_row((me + n) % NP)
        )

    def ar2_copy(n, p):
        return remote(ar2.at[p], ar2.at[p], ar2_s.at[n], ar2_r.at[p], in_column(n))

    @pl.when(is_main)
    def _():
        pieces = [parts[h:h + 1, :HD] for h in range(NH)]
        ar1[me] = jnp.concatenate(pieces + [jnp.zeros((1, HD), f32)], axis=1)
        for n in range(1, NP):
            ar1_copy(n, me).start()
        for n in range(1, NP):
            ar1_copy(n, (me + n) % NP).wait_recv()
        part = ar1[0]
        for n in range(1, NP):
            part = part + ar1[n]
        ar2[z] = part
        for n in range(1, 2 * NZ):
            ar2_copy(n, z).start()
        for n in range(1, NZ):
            ar2_copy(n, (z + n) % NZ).wait_recv()

    @pl.when(jnp.logical_not(is_main))
    def _():
        for n in range(NZ):
            ar2_copy(1, n).wait_recv()

    totals = []
    for q in range(NQ):
        part = (ar2[4 * q] + ar2[4 * q + 1]) + (ar2[4 * q + 2] + ar2[4 * q + 3])
        totals.append(part[:, :NH * HD])
    whole_sum = jnp.concatenate(totals, axis=1)
    for i in range(6):
        gg_ref[i * 128:(i + 1) * 128] = whole_sum[:, i * 128:(i + 1) * 128].reshape(128)

    for f in range(2):
        @pl.when(jnp.logical_not(stays(f)))
        def _():
            for h in range(NH):
                rp_wait(h, f).wait_recv()
    for pair in range(3):
        halves = [unfold(rp[n // NH, n % NH]) for n in (2 * pair, 2 * pair + 1)]
        out_ref[0, :, pair * 128:pair * 128 + 128] = jnp.concatenate(halves, axis=1)

    for f in range(2):
        @pl.when(jnp.logical_not(stays(f)))
        def _():
            for h in range(NH):
                p1_send(h, f).wait_send()
                rp_send(h, f).wait_send()
            q_send(f).wait_send()

            @pl.when(is_main)
            def _():
                c_send(f).wait_send()
    for h in range(NH):
        for k, (n, place, b, device) in enumerate(sends):
            ag(h, k, at(*place), b, device).wait_send()

    @pl.when(jnp.logical_not(is_main))
    def _():
        for h in range(NH):
            ac_copy(h).wait_send()

    @pl.when(is_main)
    def _():
        for n in range(1, NP):
            ar1_copy(n, me).wait_send()
        for n in range(1, 2 * NZ):
            ar2_copy(n, z).wait_send()


def local(q_in, k_in, v_in, q_gain, gate, cot):
    hbm = pl.BlockSpec(memory_space=pltpu.HBM)
    vmem = pl.BlockSpec(memory_space=pltpu.VMEM)
    dma = pltpu.SemaphoreType.DMA
    out, gg = pl.pallas_call(
        kernel,
        out_shape=(
            jax.ShapeDtypeStruct(q_in.shape, bf16),
            jax.ShapeDtypeStruct(gate.shape, f32),
        ),
        in_specs=[hbm] * 3 + [vmem] * 2 + [hbm],
        out_specs=(vmem, vmem),
        scratch_shapes=[
            pltpu.VMEM(q_in.shape, bf16),
            pltpu.VMEM(k_in.shape, bf16),
            pltpu.VMEM(v_in.shape, bf16),
            pltpu.VMEM(cot.shape, bf16),
            pltpu.VMEM((2, NH, TOK, 128), bf16),
            pltpu.VMEM((2, NH, HD, 128), bf16),
            pltpu.VMEM((2, NH, HD, 128), bf16),
            pltpu.VMEM((NH, KEYS, 128), bf16),
            pltpu.VMEM((2, NH, HD, 128), bf16),
            pltpu.VMEM((2, NH, HD, 128), bf16),
            pltpu.VMEM((NH, 2, HD, 128), bf16),
            pltpu.VMEM((NH, 2, HD, 128), bf16),
            pltpu.VMEM((2, NH, HD, 128), bf16),
            pltpu.VMEM((ROWS, KEYS), f32),
            pltpu.VMEM((ROWS, KEYS), bf16),
            pltpu.VMEM((NH, ROWS, KEYS), f32),
            pltpu.VMEM((8, 128), f32),
            pltpu.VMEM((NP, 1, 256), f32),
            pltpu.VMEM((NZ, 1, 256), f32),
            dma((4,)),
            dma((2, NH)), dma((2, NH)), dma((2,)), dma((2,)), dma((2,)), dma((2,)),
            dma((NH, 16)), dma((NH, NP, 2)), dma((NH,)), dma((NH,)),
            dma((NH, 2)), dma((2, NH)),
            dma((NP,)), dma((NP,)), dma((2 * NZ,)), dma((NZ,)),
        ],
        compiler_params=pltpu.CompilerParams(
            collective_id=0, has_side_effects=True, vmem_limit_bytes=58 * 2**20
        ),
    )(q_in, k_in, v_in, q_gain, gate, cot)
    return out, gg


def solution(mesh):
    in_specs = (
        P("dp", "seq", "segment"),
        P("dp", "seq", "segment"),
        P("dp", "seq", "segment"),
        P(),
        P(),
        P("dp", "seq", None),
    )
    out_specs = (P("dp", "seq", "segment"), P())
    return jax.shard_map(local, mesh=mesh, in_specs=in_specs, out_specs=out_specs, check_vma=False)
```

```python
import functools

import jax
import jax.numpy as jnp
from jax import lax
from jax.experimental import pallas as pl
from jax.experimental.pallas import tpu as pltpu
from jax.sharding import PartitionSpec as P

MESH = pl.DeviceIdType.MESH
HD = 64
NH = 3
TOK = 128
NZ = 16
NQ = 4
NP = 16
KEYS = 4096
ROWS = 2 * TOK
CHUNK = 4096
SCALE = HD ** (-0.5)
f32 = jnp.float32
bf16 = jnp.bfloat16


def kernel(
    q_hbm, k_hbm, v_hbm, gain_ref, gate_ref, cot_hbm,
    out_ref, gg_ref,
    q_ref, k_ref, v_ref, cot_ref,
    pack_kv, pack_q, pack_c, kv, qb, cb, ac, fo, rp, scores, probs, dprob, parts, ar1, ar2,
    load_s, p1_s, p1_r, q_s, q_r, c_s, c_r, ag_s, ag_r, ac_s, ac_r, rp_s, rp_r,
    ar1_s, ar1_r, ar2_s, ar2_r,
):
    seg = lax.axis_index("segment")
    seq = lax.axis_index("seq")
    y = lax.axis_index("dp")
    xh, c = seg // 2, seg % 2
    x, z = seq // NZ, seq % NZ
    is_main = xh == 1
    zq, zs = z // 4, z % 4
    me = (c * 4 + y) * 2 + x
    itself = z == 12 * c + y

    loads = [
        pltpu.make_async_copy(src, dst, load_s.at[n])
        for n, (src, dst) in enumerate(
            ((k_hbm, k_ref), (v_hbm, v_ref), (q_hbm, q_ref), (cot_hbm, cot_ref))
        )
    ]
    for load in loads:
        load.start()

    def target(f):
        return {"segment": xh * 2 + zq % 2, "seq": x * NZ + 4 * (2 * c + f) + y, "dp": zs}

    def source(b):
        return {"segment": xh * 2 + zq // 2, "seq": x * NZ + y + 4 * c + 8 * b, "dp": zs}

    def in_row(p):
        return {"segment": xh * 2 + p // 8, "seq": (p % 2) * NZ + z, "dp": (p // 2) % 4}

    def in_column(n):
        there = (xh * NZ + z + n) % (2 * NZ)
        return {"segment": (there // NZ) * 2 + c, "seq": x * NZ + there % NZ}

    def stays(n):
        return itself & (c == n)

    barrier = pltpu.get_barrier_semaphore()

    def hello(device):
        pl.semaphore_signal(barrier, inc=1, device_id=device, device_id_type=MESH)

    for n in range(2):
        @pl.when(jnp.logical_not(stays(n)))
        def _():
            hello(target(n))
            hello(source(n))
    for n in range(1, NP):
        hello(in_row((me + n) % NP))
    for n in range(1, 2 * NZ):
        hello(in_column(n))

    def fold(a):
        return jnp.concatenate([a[:HD], a[HD:]], axis=1)

    def unfold(a):
        return jnp.concatenate([a[:, :HD], a[:, HD:]], axis=0)

    for load in loads:
        load.wait()
    for pair in range(3):
        cols = slice(pair * 128, pair * 128 + 128)
        kt, vt, qt = k_ref[0, :, cols], v_ref[0, :, cols], q_ref[0, :, cols]
        ct = cot_ref[0, :, pl.ds(pl.multiple_of(c * 384 + pair * 128, 128), 128)]
        for half in range(2):
            f, h = (2 * pair + half) // NH, (2 * pair + half) % NH
            lanes = slice(half * HD, half * HD + HD)
            pack_kv[f, h] = jnp.concatenate([kt[:, lanes], vt[:, lanes]], axis=1)
            pack_q[f, h] = fold(qt[:, lanes])
            pack_c[f, h] = fold(ct[:, lanes])

    def rows(p, b):
        return pl.ds(pl.multiple_of((p * 2 + b) * TOK, TOK), TOK)

    def whole(p):
        return pl.ds(pl.multiple_of(p * ROWS, ROWS), ROWS)

    def remote(src, dst, send, recv, device):
        return pltpu.make_async_remote_copy(
            src_ref=src, dst_ref=dst, send_sem=send, recv_sem=recv,
            device_id=device, device_id_type=MESH,
        )

    there = ((zq % 2) * 4 + zs) * 2 + x
    block = zq // 2

    def p1_send(h, f):
        return remote(
            pack_kv.at[f, h], kv.at[h, rows(there, block)], p1_s.at[f, h], p1_r.at[block, h],
            target(f),
        )

    def p1_wait(h, b):
        return remote(
            pack_kv.at[0, h], kv.at[h, rows(me, b)], p1_s.at[0, h], p1_r.at[b, h], source(b)
        )

    def q_send(f):
        return remote(pack_q.at[f], qb.at[block], q_s.at[f], q_r.at[block], target(f))

    def q_wait(b):
        return remote(pack_q.at[0], qb.at[b], q_s.at[0], q_r.at[b], source(b))

    def c_send(f):
        return remote(pack_c.at[f], cb.at[block], c_s.at[f], c_r.at[block], target(f))

    def c_wait(b):
        return remote(pack_c.at[0], cb.at[b], c_s.at[0], c_r.at[b], source(b))

    pl.semaphore_wait(barrier, 50 - 2 * itself.astype(jnp.int32))

    for h in range(NH):
        for n in range(2):
            f = (n + z) % 2

            @pl.when(jnp.logical_not(stays(f)))
            def _():
                p1_send(h, f).start()
        if h == NH - 1:
            for n in range(2):
                f = (n + z) % 2

                @pl.when(jnp.logical_not(stays(f)))
                def _():
                    q_send(f).start()
    for f in range(2):
        @pl.when(stays(f))
        def _():
            for h in range(NH):
                kv[h, rows(me, f)] = pack_kv[f, h]
            qb[f] = pack_q[f]
            cb[f] = pack_c[f]

    over_x = {"seq": (1 - x) * NZ + z}
    up, down = {"dp": (y + 1) % 4}, {"dp": (y + 3) % 4}
    sibling = {"segment": xh * 2 + 1 - c}

    def at(dy, dx):
        return (c * 4 + (y + dy) % 4) * 2 + (x + dx) % 2

    def ag(h, k, p, b, device):
        where = whole(p) if b is None else rows(p, b)
        return remote(
            kv.at[h, where], kv.at[h, where], ag_s.at[h, k], ag_r.at[h, p, b or 0], device
        )

    def beside(h, k, core, dy):
        p = (core * 4 + (y + dy) % 4) * 2
        where = pl.ds(pl.multiple_of(p * ROWS, 2 * ROWS), 2 * ROWS)
        return remote(
            kv.at[h, where], kv.at[h, where], ag_s.at[h, k], ag_r.at[h, p, 0], sibling
        )

    def arrived(h, p, b=None):
        ag(h, 0, p, b, over_x).wait_recv()

    sends = (
        (0, (0, 0), None, over_x), (0, (0, 0), None, up), (0, (0, 0), None, down),
        (1, (0, 1), None, up), (1, (0, 1), None, down),
        (2, (1, 0), 0, down), (3, (3, 0), 1, up),
        (6, (2, 0), None, over_x),
    )
    places = {1: (0, 1), 2: (1, 0), 3: (3, 0), 4: (1, 1), 5: (3, 1), 7: (2, 1)}
    siblings = {1: (8, 0), 4: (9, 1), 5: (10, 3), 7: (11, 2)}

    def stage(h, number):
        if number == 0:
            for b in range(2):
                @pl.when(jnp.logical_not(stays(b)))
                def _():
                    p1_wait(h, b).wait_recv()
        elif number == 6:
            arrived(h, at(2, 0), 0)
            arrived(h, at(2, 0), 1)
        else:
            arrived(h, at(*places[number]))
        for k, (n, place, b, device) in enumerate(sends):
            if n == number:
                ag(h, k, at(*place), b, device).start()
        if number in siblings:
            k, dy = siblings[number]
            beside(h, k, c, dy).start()

    zero_half = jnp.zeros((ROWS, HD), bf16)

    def both(ref, h):
        return jnp.concatenate([unfold(ref[0, h]), unfold(ref[1, h])], axis=0)

    def base_of(h, row):
        raw = both(qb, h).astype(f32)
        unit = raw * lax.rsqrt(jnp.mean(raw * raw, axis=-1, keepdims=True) + 1e-06)
        return unit * gain_ref[row:row + 1, :]

    def forward(h, query, keep):
        wide = jnp.concatenate([query * jnp.asarray(SCALE, bf16), zero_half], axis=1)
        s = lax.dot_general(wide, kv[h], (((1,), (1,)), ((), ())), preferred_element_type=f32)
        scores[...] = s
        top = s[:, :128]
        for i in range(1, KEYS // 128):
            top = jnp.maximum(top, s[:, i * 128:(i + 1) * 128])
        peak = jnp.max(top, axis=-1, keepdims=True)
        e = jnp.exp(scores[...] - peak)
        total = e[:, :128]
        for i in range(1, KEYS // 128):
            total = total + e[:, i * 128:(i + 1) * 128]
        p = e.astype(bf16)
        if keep:
            probs[...] = p
        acc = jnp.dot(p, kv[h], preferred_element_type=f32)
        total = jnp.sum(total, axis=-1, keepdims=True)
        return acc[:, HD:] / total, total

    def ac_copy(h):
        return remote(
            fo.at[h], ac.at[h], ac_s.at[h], ac_r.at[h], {"segment": (1 - xh) * 2 + c}
        )

    def rp_send(h, b):
        return remote(
            fo.at[h, b], rp.at[zq % 2, h], rp_s.at[h, b], rp_r.at[zq % 2, h], source(b)
        )

    def rp_wait(h, f):
        return remote(fo.at[h, 0], rp.at[f, h], rp_s.at[h, 0], rp_r.at[f, h], target(f))

    def give_back(h):
        for b in range(2):
            @pl.when(jnp.logical_not(stays(b)))
            def _():
                rp_send(h, b).start()

            @pl.when(stays(b))
            def _():
                rp[b, h] = fo[h, b]

    def keep_out(h, normed):
        fo[h, 0] = fold(normed[:TOK].astype(bf16))
        fo[h, 1] = fold(normed[TOK:].astype(bf16))

    def control_head(h):
        normed, _ = forward(h, base_of(h, 0).astype(bf16), False)
        keep_out(h, normed)
        ac_copy(h).start()
        give_back(h)

    def dprob_head(h):
        wide = jnp.concatenate([zero_half, both(cb, h)], axis=1)
        dprob[h] = lax.dot_general(
            wide, kv[h], (((1,), (1,)), ((), ())), preferred_element_type=f32
        )

    def main_head(h):
        base = base_of(h, 1)
        first = zq * (NH * HD) + h * HD
        tile = gate_ref[pl.ds(pl.multiple_of((first // 128) * 128, 128), 128)].reshape(1, 128)
        gate = jnp.where((zq + h) % 2 == 1, tile[:, HD:], tile[:, :HD])
        ac_copy(h).wait_recv()
        first_wide = jnp.concatenate([unfold(ac[h, 0]), unfold(ac[h, 1])], axis=0).astype(f32)
        residual = (gate * first_wide).astype(bf16)
        query = (base + residual.astype(f32)).astype(bf16)
        normed, total = forward(h, query, True)
        keep_out(h, normed)
        give_back(h)
        upstream = both(cb, h)
        delta = jnp.sum(upstream.astype(f32) * normed, axis=-1, keepdims=True)
        inverse = 1.0 / total
        ds = (probs[...].astype(f32) * inverse * (dprob[h] - delta)).astype(bf16)
        acc = jnp.dot(ds, kv[h], preferred_element_type=f32)
        rgrad = (acc[:, :HD] * SCALE).astype(bf16).astype(f32)
        part = jnp.sum(first_wide * rgrad, axis=0, keepdims=True)
        parts[pl.ds(h, 1), :] = jnp.concatenate([part, part], axis=1)

    def complete(h):
        for dy in range(4):
            beside(h, 0, 1 - c, dy).wait_recv()

    def stages(h, *numbers):
        for n in numbers:
            stage(h, n)

    stages(0, 0, 1, 2, 3)
    stages(1, 0)
    stages(0, 4, 5, 6)
    stages(1, 1, 2, 3)
    stages(2, 0)
    for f in range(2):
        @pl.when(is_main & jnp.logical_not(stays(f)))
        def _():
            c_send(f).start()
    for b in range(2):
        @pl.when(jnp.logical_not(stays(b)))
        def _():
            q_wait(b).wait_recv()
    stages(1, 4, 5, 6)
    stages(0, 7)
    complete(0)

    @pl.when(is_main)
    def _():
        stages(2, 1, 2, 3)
        stages(1, 7)
        for b in range(2):
            @pl.when(jnp.logical_not(stays(b)))
            def _():
                c_wait(b).wait_recv()
        complete(1)

        def ahead(h, carry):
            dprob_head(h)
            return carry

        lax.fori_loop(0, 2, ahead, 0)

    def heads(h, carry):
        @pl.when(jnp.logical_not(is_main))
        def _():
            @pl.when(h == 1)
            def _():
                stages(2, 1, 2, 3)
                stages(1, 7)
                complete(1)

            @pl.when(h == 2)
            def _():
                stages(2, 4, 5, 6, 7)
                complete(2)

            control_head(h)

        @pl.when(is_main)
        def _():
            @pl.when(h == 1)
            def _():
                stages(2, 4, 5, 6)

            @pl.when(h == 2)
            def _():
                stages(2, 7)
                complete(2)
                dprob_head(2)

            main_head(h)
        return carry

    lax.fori_loop(0, NH, heads, 0)

    def ar1_copy(n, p):
        return remote(
            ar1.at[p], ar1.at[p], ar1_s.at[n], ar1_r.at[p], in_row((me + n) % NP)
        )

    def ar2_copy(n, p):
        return remote(ar2.at[p], ar2.at[p], ar2_s.at[n], ar2_r.at[p], in_column(n))

    @pl.when(is_main)
    def _():
        pieces = [parts[h:h + 1, :HD] for h in range(NH)]
        ar1[me] = jnp.concatenate(pieces + [jnp.zeros((1, HD), f32)], axis=1)
        for n in range(1, NP):
            ar1_copy(n, me).start()
        for n in range(1, NP):
            ar1_copy(n, (me + n) % NP).wait_recv()
        part = ar1[0]
        for n in range(1, NP):
            part = part + ar1[n]
        ar2[z] = part
        for n in range(1, 2 * NZ):
            ar2_copy(n, z).start()
        for n in range(1, NZ):
            ar2_copy(n, (z + n) % NZ).wait_recv()

    @pl.when(jnp.logical_not(is_main))
    def _():
        for n in range(NZ):
            ar2_copy(1, n).wait_recv()

    totals = []
    for q in range(NQ):
        part = (ar2[4 * q] + ar2[4 * q + 1]) + (ar2[4 * q + 2] + ar2[4 * q + 3])
        totals.append(part[:, :NH * HD])
    whole_sum = jnp.concatenate(totals, axis=1)
    for i in range(6):
        gg_ref[i * 128:(i + 1) * 128] = whole_sum[:, i * 128:(i + 1) * 128].reshape(128)

    for f in range(2):
        @pl.when(jnp.logical_not(stays(f)))
        def _():
            for h in range(NH):
                rp_wait(h, f).wait_recv()
    for pair in range(3):
        halves = [unfold(rp[n // NH, n % NH]) for n in (2 * pair, 2 * pair + 1)]
        out_ref[0, :, pair * 128:pair * 128 + 128] = jnp.concatenate(halves, axis=1)

    for f in range(2):
        @pl.when(jnp.logical_not(stays(f)))
        def _():
            for h in range(NH):
                p1_send(h, f).wait_send()
                rp_send(h, f).wait_send()
            q_send(f).wait_send()

            @pl.when(is_main)
            def _():
                c_send(f).wait_send()
    for h in range(NH):
        for k, (n, place, b, device) in enumerate(sends):
            ag(h, k, at(*place), b, device).wait_send()
        for k, dy in siblings.values():
            beside(h, k, c, dy).wait_send()

    @pl.when(jnp.logical_not(is_main))
    def _():
        for h in range(NH):
            ac_copy(h).wait_send()

    @pl.when(is_main)
    def _():
        for n in range(1, NP):
            ar1_copy(n, me).wait_send()
        for n in range(1, 2 * NZ):
            ar2_copy(n, z).wait_send()


def local(q_in, k_in, v_in, q_gain, gate, cot):
    hbm = pl.BlockSpec(memory_space=pltpu.HBM)
    vmem = pl.BlockSpec(memory_space=pltpu.VMEM)
    dma = pltpu.SemaphoreType.DMA
    out, gg = pl.pallas_call(
        kernel,
        out_shape=(
            jax.ShapeDtypeStruct(q_in.shape, bf16),
            jax.ShapeDtypeStruct(gate.shape, f32),
        ),
        in_specs=[hbm] * 3 + [vmem] * 2 + [hbm],
        out_specs=(vmem, vmem),
        scratch_shapes=[
            pltpu.VMEM(q_in.shape, bf16),
            pltpu.VMEM(k_in.shape, bf16),
            pltpu.VMEM(v_in.shape, bf16),
            pltpu.VMEM(cot.shape, bf16),
            pltpu.VMEM((2, NH, TOK, 128), bf16),
            pltpu.VMEM((2, NH, HD, 128), bf16),
            pltpu.VMEM((2, NH, HD, 128), bf16),
            pltpu.VMEM((NH, KEYS, 128), bf16),
            pltpu.VMEM((2, NH, HD, 128), bf16),
            pltpu.VMEM((2, NH, HD, 128), bf16),
            pltpu.VMEM((NH, 2, HD, 128), bf16),
            pltpu.VMEM((NH, 2, HD, 128), bf16),
            pltpu.VMEM((2, NH, HD, 128), bf16),
            pltpu.VMEM((ROWS, KEYS), f32),
            pltpu.VMEM((ROWS, KEYS), bf16),
            pltpu.VMEM((NH, ROWS, KEYS), f32),
            pltpu.VMEM((8, 128), f32),
            pltpu.VMEM((NP, 1, 256), f32),
            pltpu.VMEM((NZ, 1, 256), f32),
            dma((4,)),
            dma((2, NH)), dma((2, NH)), dma((2,)), dma((2,)), dma((2,)), dma((2,)),
            dma((NH, 16)), dma((NH, NP, 2)), dma((NH,)), dma((NH,)),
            dma((NH, 2)), dma((2, NH)),
            dma((NP,)), dma((NP,)), dma((2 * NZ,)), dma((NZ,)),
        ],
        compiler_params=pltpu.CompilerParams(
            collective_id=0, has_side_effects=True, vmem_limit_bytes=58 * 2**20
        ),
    )(q_in, k_in, v_in, q_gain, gate, cot)
    return out, gg


def solution(mesh):
    in_specs = (
        P("dp", "seq", "segment"),
        P("dp", "seq", "segment"),
        P("dp", "seq", "segment"),
        P(),
        P(),
        P("dp", "seq", None),
    )
    out_specs = (P("dp", "seq", "segment"), P())
    return jax.shard_map(local, mesh=mesh, in_specs=in_specs, out_specs=out_specs, check_vma=False)
```

```python
import functools

import jax
import jax.numpy as jnp
from jax import lax
from jax.experimental import pallas as pl
from jax.experimental.pallas import tpu as pltpu
from jax.sharding import PartitionSpec as P

MESH = pl.DeviceIdType.MESH
HD = 64
NH = 3
TOK = 128
NZ = 16
NQ = 4
NP = 16
KEYS = 4096
ROWS = 2 * TOK
CHUNK = 4096
SCALE = HD ** (-0.5)
f32 = jnp.float32
bf16 = jnp.bfloat16


def kernel(
    q_hbm, k_hbm, v_hbm, gain_ref, gate_ref, cot_hbm,
    out_ref, gg_ref,
    q_ref, k_ref, v_ref, cot_ref, out_v, out_s,
    pack_kv, pack_q, pack_c, kv, qb, cb, ac, fo, rp, scores, probs, dprob, parts, ar1, ar2,
    load_s, p1_s, p1_r, q_s, q_r, c_s, c_r, ag_s, ag_r, ac_s, ac_r, rp_s, rp_r,
    ar1_s, ar1_r, ar2_s, ar2_r,
):
    seg = lax.axis_index("segment")
    seq = lax.axis_index("seq")
    y = lax.axis_index("dp")
    xh, c = seg // 2, seg % 2
    x, z = seq // NZ, seq % NZ
    is_main = xh == 1
    zq, zs = z // 4, z % 4
    me = (c * 4 + y) * 2 + x
    itself = z == 12 * c + y

    loads = [
        pltpu.make_async_copy(src, dst, load_s.at[n])
        for n, (src, dst) in enumerate(
            ((k_hbm, k_ref), (v_hbm, v_ref), (q_hbm, q_ref), (cot_hbm, cot_ref))
        )
    ]
    for load in loads:
        load.start()

    def target(f):
        return {"segment": xh * 2 + zq % 2, "seq": x * NZ + 4 * (2 * c + f) + y, "dp": zs}

    def source(b):
        return {"segment": xh * 2 + zq // 2, "seq": x * NZ + y + 4 * c + 8 * b, "dp": zs}

    def in_row(p):
        return {"segment": xh * 2 + p // 8, "seq": (p % 2) * NZ + z, "dp": (p // 2) % 4}

    def in_column(n):
        there = (xh * NZ + z + n) % (2 * NZ)
        return {"segment": (there // NZ) * 2 + c, "seq": x * NZ + there % NZ}

    def stays(n):
        return itself & (c == n)

    barrier = pltpu.get_barrier_semaphore()

    def hello(device):
        pl.semaphore_signal(barrier, inc=1, device_id=device, device_id_type=MESH)

    for n in range(2):
        @pl.when(jnp.logical_not(stays(n)))
        def _():
            hello(target(n))
            hello(source(n))
    for n in range(1, NP):
        hello(in_row((me + n) % NP))
    for n in range(1, 2 * NZ):
        hello(in_column(n))

    def fold(a):
        return jnp.concatenate([a[:HD], a[HD:]], axis=1)

    def unfold(a):
        return jnp.concatenate([a[:, :HD], a[:, HD:]], axis=0)

    for load in loads:
        load.wait()
    for pair in range(3):
        cols = slice(pair * 128, pair * 128 + 128)
        kt, vt, qt = k_ref[0, :, cols], v_ref[0, :, cols], q_ref[0, :, cols]
        ct = cot_ref[0, :, pl.ds(pl.multiple_of(c * 384 + pair * 128, 128), 128)]
        for half in range(2):
            f, h = (2 * pair + half) // NH, (2 * pair + half) % NH
            lanes = slice(half * HD, half * HD + HD)
            pack_kv[f, h] = jnp.concatenate([kt[:, lanes], vt[:, lanes]], axis=1)
            pack_q[f, h] = fold(qt[:, lanes])
            pack_c[f, h] = fold(ct[:, lanes])

    def rows(p, b):
        return pl.ds(pl.multiple_of((p * 2 + b) * TOK, TOK), TOK)

    def whole(p):
        return pl.ds(pl.multiple_of(p * ROWS, ROWS), ROWS)

    def remote(src, dst, send, recv, device):
        return pltpu.make_async_remote_copy(
            src_ref=src, dst_ref=dst, send_sem=send, recv_sem=recv,
            device_id=device, device_id_type=MESH,
        )

    there = ((zq % 2) * 4 + zs) * 2 + x
    block = zq // 2

    def p1_send(h, f):
        return remote(
            pack_kv.at[f, h], kv.at[h, rows(there, block)], p1_s.at[f, h], p1_r.at[block, h],
            target(f),
        )

    def p1_wait(h, b):
        return remote(
            pack_kv.at[0, h], kv.at[h, rows(me, b)], p1_s.at[0, h], p1_r.at[b, h], source(b)
        )

    def q_send(f):
        return remote(pack_q.at[f], qb.at[block], q_s.at[f], q_r.at[block], target(f))

    def q_wait(b):
        return remote(pack_q.at[0], qb.at[b], q_s.at[0], q_r.at[b], source(b))

    def c_send(f):
        return remote(pack_c.at[f], cb.at[block], c_s.at[f], c_r.at[block], target(f))

    def c_wait(b):
        return remote(pack_c.at[0], cb.at[b], c_s.at[0], c_r.at[b], source(b))

    pl.semaphore_wait(barrier, 50 - 2 * itself.astype(jnp.int32))

    for h in range(NH):
        for n in range(2):
            f = (n + z) % 2

            @pl.when(jnp.logical_not(stays(f)))
            def _():
                p1_send(h, f).start()
        if h == NH - 1:
            for n in range(2):
                f = (n + z) % 2

                @pl.when(jnp.logical_not(stays(f)))
                def _():
                    q_send(f).start()
    for f in range(2):
        @pl.when(stays(f))
        def _():
            for h in range(NH):
                kv[h, rows(me, f)] = pack_kv[f, h]
            qb[f] = pack_q[f]
            cb[f] = pack_c[f]

    over_x = {"seq": (1 - x) * NZ + z}
    up, down = {"dp": (y + 1) % 4}, {"dp": (y + 3) % 4}
    sibling = {"segment": xh * 2 + 1 - c}

    def at(dy, dx):
        return (c * 4 + (y + dy) % 4) * 2 + (x + dx) % 2

    def ag(h, k, p, b, device):
        where = whole(p) if b is None else rows(p, b)
        return remote(
            kv.at[h, where], kv.at[h, where], ag_s.at[h, k], ag_r.at[h, p, b or 0], device
        )

    def beside(h, k, core, dy):
        p = (core * 4 + (y + dy) % 4) * 2
        where = pl.ds(pl.multiple_of(p * ROWS, 2 * ROWS), 2 * ROWS)
        return remote(
            kv.at[h, where], kv.at[h, where], ag_s.at[h, k], ag_r.at[h, p, 0], sibling
        )

    def arrived(h, p, b=None):
        ag(h, 0, p, b, over_x).wait_recv()

    sends = (
        (0, (0, 0), None, over_x), (0, (0, 0), None, up), (0, (0, 0), None, down),
        (1, (0, 1), None, up), (1, (0, 1), None, down),
        (2, (1, 0), 0, down), (3, (3, 0), 1, up),
        (6, (2, 0), None, over_x),
    )
    places = {1: (0, 1), 2: (1, 0), 3: (3, 0), 4: (1, 1), 5: (3, 1), 7: (2, 1)}
    siblings = {1: (8, 0), 4: (9, 1), 5: (10, 3), 7: (11, 2)}

    def stage(h, number):
        if number == 0:
            for b in range(2):
                @pl.when(jnp.logical_not(stays(b)))
                def _():
                    p1_wait(h, b).wait_recv()
        elif number == 6:
            arrived(h, at(2, 0), 0)
            arrived(h, at(2, 0), 1)
        else:
            arrived(h, at(*places[number]))
        for k, (n, place, b, device) in enumerate(sends):
            if n == number:
                ag(h, k, at(*place), b, device).start()
        if number in siblings:
            k, dy = siblings[number]
            beside(h, k, c, dy).start()

    zero_half = jnp.zeros((ROWS, HD), bf16)

    def both(ref, h):
        return jnp.concatenate([unfold(ref[0, h]), unfold(ref[1, h])], axis=0)

    def base_of(h, row):
        raw = both(qb, h).astype(f32)
        unit = raw * lax.rsqrt(jnp.mean(raw * raw, axis=-1, keepdims=True) + 1e-06)
        return unit * gain_ref[row:row + 1, :]

    def forward(h, query, keep):
        wide = jnp.concatenate([query * jnp.asarray(SCALE, bf16), zero_half], axis=1)
        s = lax.dot_general(wide, kv[h], (((1,), (1,)), ((), ())), preferred_element_type=f32)
        scores[...] = s
        top = s[:, :128]
        for i in range(1, KEYS // 128):
            top = jnp.maximum(top, s[:, i * 128:(i + 1) * 128])
        peak = jnp.max(top, axis=-1, keepdims=True)
        e = jnp.exp(scores[...] - peak)
        total = e[:, :128]
        for i in range(1, KEYS // 128):
            total = total + e[:, i * 128:(i + 1) * 128]
        p = e.astype(bf16)
        if keep:
            probs[...] = p
        acc = jnp.dot(p, kv[h], preferred_element_type=f32)
        total = jnp.sum(total, axis=-1, keepdims=True)
        return acc[:, HD:] / total, total

    def ac_copy(h):
        return remote(
            fo.at[h], ac.at[h], ac_s.at[h], ac_r.at[h], {"segment": (1 - xh) * 2 + c}
        )

    def rp_send(h, b):
        return remote(
            fo.at[h, b], rp.at[zq % 2, h], rp_s.at[h, b], rp_r.at[zq % 2, h], source(b)
        )

    def rp_wait(h, f):
        return remote(fo.at[h, 0], rp.at[f, h], rp_s.at[h, 0], rp_r.at[f, h], target(f))

    def give_back(h):
        for b in range(2):
            @pl.when(jnp.logical_not(stays(b)))
            def _():
                rp_send(h, b).start()

            @pl.when(stays(b))
            def _():
                rp[b, h] = fo[h, b]

    def keep_out(h, normed):
        fo[h, 0] = fold(normed[:TOK].astype(bf16))
        fo[h, 1] = fold(normed[TOK:].astype(bf16))

    def control_head(h):
        normed, _ = forward(h, base_of(h, 0).astype(bf16), False)
        keep_out(h, normed)
        ac_copy(h).start()
        give_back(h)

    def dprob_head(h):
        wide = jnp.concatenate([zero_half, both(cb, h)], axis=1)
        dprob[h] = lax.dot_general(
            wide, kv[h], (((1,), (1,)), ((), ())), preferred_element_type=f32
        )

    def main_head(h):
        base = base_of(h, 1)
        first = zq * (NH * HD) + h * HD
        tile = gate_ref[pl.ds(pl.multiple_of((first // 128) * 128, 128), 128)].reshape(1, 128)
        gate = jnp.where((zq + h) % 2 == 1, tile[:, HD:], tile[:, :HD])
        ac_copy(h).wait_recv()
        first_wide = jnp.concatenate([unfold(ac[h, 0]), unfold(ac[h, 1])], axis=0).astype(f32)
        residual = (gate * first_wide).astype(bf16)
        query = (base + residual.astype(f32)).astype(bf16)
        normed, total = forward(h, query, True)
        keep_out(h, normed)
        give_back(h)
        upstream = both(cb, h)
        delta = jnp.sum(upstream.astype(f32) * normed, axis=-1, keepdims=True)
        inverse = 1.0 / total
        ds = (probs[...].astype(f32) * inverse * (dprob[h] - delta)).astype(bf16)
        acc = jnp.dot(ds, kv[h], preferred_element_type=f32)
        rgrad = (acc[:, :HD] * SCALE).astype(bf16).astype(f32)
        part = jnp.sum(first_wide * rgrad, axis=0, keepdims=True)
        parts[pl.ds(h, 1), :] = jnp.concatenate([part, part], axis=1)

    def complete(h):
        for dy in range(4):
            beside(h, 0, 1 - c, dy).wait_recv()

    def stages(h, *numbers):
        for n in numbers:
            stage(h, n)

    stages(0, 0, 1, 2, 3)
    stages(1, 0)
    stages(0, 4, 5, 6)
    stages(1, 1, 2, 3)
    stages(2, 0)
    for f in range(2):
        @pl.when(is_main & jnp.logical_not(stays(f)))
        def _():
            c_send(f).start()
    for b in range(2):
        @pl.when(jnp.logical_not(stays(b)))
        def _():
            q_wait(b).wait_recv()
    stages(1, 4, 5, 6)
    stages(0, 7)
    complete(0)

    @pl.when(is_main)
    def _():
        stages(2, 1, 2, 3)
        stages(1, 7)
        for b in range(2):
            @pl.when(jnp.logical_not(stays(b)))
            def _():
                c_wait(b).wait_recv()
        complete(1)

        def ahead(h, carry):
            dprob_head(h)
            return carry

        lax.fori_loop(0, 2, ahead, 0)

    def heads(h, carry):
        @pl.when(jnp.logical_not(is_main))
        def _():
            @pl.when(h == 1)
            def _():
                stages(2, 1, 2, 3)
                stages(1, 7)
                complete(1)

            @pl.when(h == 2)
            def _():
                stages(2, 4, 5, 6, 7)
                complete(2)

            control_head(h)

        @pl.when(is_main)
        def _():
            @pl.when(h == 1)
            def _():
                stages(2, 4, 5, 6)

            @pl.when(h == 2)
            def _():
                stages(2, 7)
                complete(2)
                dprob_head(2)

            main_head(h)
        return carry

    lax.fori_loop(0, NH, heads, 0)

    def ar1_copy(n, p):
        return remote(
            ar1.at[p], ar1.at[p], ar1_s.at[n], ar1_r.at[p], in_row((me + n) % NP)
        )

    def ar2_copy(n, p):
        return remote(ar2.at[p], ar2.at[p], ar2_s.at[n], ar2_r.at[p], in_column(n))

    @pl.when(is_main)
    def _():
        pieces = [parts[h:h + 1, :HD] for h in range(NH)]
        ar1[me] = jnp.concatenate(pieces + [jnp.zeros((1, HD), f32)], axis=1)
        for n in range(1, NP):
            ar1_copy(n, me).start()
        for n in range(1, NP):
            ar1_copy(n, (me + n) % NP).wait_recv()
        part = ar1[0]
        for n in range(1, NP):
            part = part + ar1[n]
        ar2[z] = part
        for n in range(1, 2 * NZ):
            ar2_copy(n, z).start()

    for f in range(2):
        @pl.when(jnp.logical_not(stays(f)))
        def _():
            for h in range(NH):
                rp_wait(h, f).wait_recv()
    for pair in range(3):
        halves = [unfold(rp[n // NH, n % NH]) for n in (2 * pair, 2 * pair + 1)]
        out_v[0, :, pair * 128:pair * 128 + 128] = jnp.concatenate(halves, axis=1)

    out_copy = pltpu.make_async_copy(out_v, out_ref, out_s)
    out_copy.start()

    @pl.when(is_main)
    def _():
        for n in range(1, NZ):
            ar2_copy(n, (z + n) % NZ).wait_recv()

    @pl.when(jnp.logical_not(is_main))
    def _():
        for n in range(NZ):
            ar2_copy(1, n).wait_recv()

    totals = []
    for q in range(NQ):
        part = (ar2[4 * q] + ar2[4 * q + 1]) + (ar2[4 * q + 2] + ar2[4 * q + 3])
        totals.append(part[:, :NH * HD])
    whole_sum = jnp.concatenate(totals, axis=1)
    for i in range(6):
        gg_ref[i * 128:(i + 1) * 128] = whole_sum[:, i * 128:(i + 1) * 128].reshape(128)

    out_copy.wait()
    for f in range(2):
        @pl.when(jnp.logical_not(stays(f)))
        def _():
            for h in range(NH):
                p1_send(h, f).wait_send()
                rp_send(h, f).wait_send()
            q_send(f).wait_send()

            @pl.when(is_main)
            def _():
                c_send(f).wait_send()
    for h in range(NH):
        for k, (n, place, b, device) in enumerate(sends):
            ag(h, k, at(*place), b, device).wait_send()
        for k, dy in siblings.values():
            beside(h, k, c, dy).wait_send()

    @pl.when(jnp.logical_not(is_main))
    def _():
        for h in range(NH):
            ac_copy(h).wait_send()

    @pl.when(is_main)
    def _():
        for n in range(1, NP):
            ar1_copy(n, me).wait_send()
        for n in range(1, 2 * NZ):
            ar2_copy(n, z).wait_send()


def local(q_in, k_in, v_in, q_gain, gate, cot):
    hbm = pl.BlockSpec(memory_space=pltpu.HBM)
    vmem = pl.BlockSpec(memory_space=pltpu.VMEM)
    dma = pltpu.SemaphoreType.DMA
    out, gg = pl.pallas_call(
        kernel,
        out_shape=(
            jax.ShapeDtypeStruct(q_in.shape, bf16),
            jax.ShapeDtypeStruct(gate.shape, f32),
        ),
        in_specs=[hbm] * 3 + [vmem] * 2 + [hbm],
        out_specs=(hbm, vmem),
        scratch_shapes=[
            pltpu.VMEM(q_in.shape, bf16),
            pltpu.VMEM(k_in.shape, bf16),
            pltpu.VMEM(v_in.shape, bf16),
            pltpu.VMEM(cot.shape, bf16),
            pltpu.VMEM(q_in.shape, bf16),
            pltpu.SemaphoreType.DMA,
            pltpu.VMEM((2, NH, TOK, 128), bf16),
            pltpu.VMEM((2, NH, HD, 128), bf16),
            pltpu.VMEM((2, NH, HD, 128), bf16),
            pltpu.VMEM((NH, KEYS, 128), bf16),
            pltpu.VMEM((2, NH, HD, 128), bf16),
            pltpu.VMEM((2, NH, HD, 128), bf16),
            pltpu.VMEM((NH, 2, HD, 128), bf16),
            pltpu.VMEM((NH, 2, HD, 128), bf16),
            pltpu.VMEM((2, NH, HD, 128), bf16),
            pltpu.VMEM((ROWS, KEYS), f32),
            pltpu.VMEM((ROWS, KEYS), bf16),
            pltpu.VMEM((NH, ROWS, KEYS), f32),
            pltpu.VMEM((8, 128), f32),
            pltpu.VMEM((NP, 1, 256), f32),
            pltpu.VMEM((NZ, 1, 256), f32),
            dma((4,)),
            dma((2, NH)), dma((2, NH)), dma((2,)), dma((2,)), dma((2,)), dma((2,)),
            dma((NH, 16)), dma((NH, NP, 2)), dma((NH,)), dma((NH,)),
            dma((NH, 2)), dma((2, NH)),
            dma((NP,)), dma((NP,)), dma((2 * NZ,)), dma((NZ,)),
        ],
        compiler_params=pltpu.CompilerParams(
            collective_id=0, has_side_effects=True, vmem_limit_bytes=58 * 2**20
        ),
    )(q_in, k_in, v_in, q_gain, gate, cot)
    return out, gg


def solution(mesh):
    in_specs = (
        P("dp", "seq", "segment"),
        P("dp", "seq", "segment"),
        P("dp", "seq", "segment"),
        P(),
        P(),
        P("dp", "seq", None),
    )
    out_specs = (P("dp", "seq", "segment"), P())
    return jax.shard_map(local, mesh=mesh, in_specs=in_specs, out_specs=out_specs, check_vma=False)
```
